768 devices in a mesh: row: 8 (over y_hi, core), col: 96 (over y_lo, z, x).
Axes of the slice: x: 4, y: 8 (y_hi: 4, y_lo: 2; y = y_hi * 2 + y_lo), z: 12, core: 2. Of those that a mesh axis runs over, the one named last changes fastest.
Arguments:
- tokens: bfloat16 [192, 8192], P('col', 'row'), may hold values from -64 to 64
- norm_gain: float32 [8192], P('row'), may hold values from 0.1 to 1.9
- w_gate: bfloat16 [8192, 24576], P('row', 'col'), may hold values from -0.0625 to 0.0625
- w_up: bfloat16 [8192, 24576], P('row', 'col'), may hold values from -0.0625 to 0.0625
- w_down: bfloat16 [24576, 8192], P('col', 'row'), may hold values from -0.109375 to 0.109375
Outputs:
- mixed: bfloat16 [192, 8192], P('col', 'row')
The draws below stay inside these ranges and needn't reach their ends.
All inputs are finite; a program needn't handle non-finite values.
Results may differ from the reference program's by a relative error of at most 0.02.
Values may be sent and summed in bfloat16 or wider, within the bound.
No kernel may reach another device: no remote copies, remote signals or barrier semaphores. Data moves between devices by JAX's collectives and lax.ppermute only.
A program may use at most 32 MiB of HBM per device.

```python
import math
import jax
import jax.numpy as jnp
from jax import lax

D = 8192
FF = 24576
TOKENS = 192
ITERS = 2


def draw_tokens(key, part):
    first, second, third = jax.random.split(key, 3)
    place = jnp.arange(D, dtype=jnp.float32) / D
    base = jnp.clip(jax.random.normal(first, (TOKENS, D), jnp.float32), -6.0, 6.0)
    ramp = 0.5 + place
    column = 0.35 * jnp.exp(jax.random.uniform(second, (D,), jnp.float32, 0.0, math.log(10.0)))
    rowscale = jnp.exp(jax.random.uniform(third, (TOKENS, 1), jnp.float32, -0.7, 0.7))
    return (base * column * ramp * rowscale).astype(jnp.bfloat16)


def levels(stream_key, shape, shards, low, top_value):
    level = 1.0
    for dim, parts in shards:
        steps = jax.random.uniform(jax.random.fold_in(jax.random.fold_in(stream_key, 6), dim), (parts,), jnp.float32, low / len(shards), top_value / len(shards))
        level = level * jnp.repeat(jnp.exp(steps), shape[dim] // parts).reshape((-1,) + (1,) * (len(shape) - 1 - dim))
    return level


def bell_draw(stream_key, dims, width, limit, cuts=(), kind=jnp.bfloat16):
    result = jax.random.normal(stream_key, dims, jnp.float32) * width
    if len(cuts) > 0:
        result = levels(stream_key, dims, cuts, -0.22, 0.18) * result
    return jnp.clip(result, min=-limit, max=limit).astype(kind)


def setup_inputs(seed: int = 0) -> dict:
    keys = jax.random.split(jax.random.key(seed), 6)
    return {
        "tokens": draw_tokens(jax.random.fold_in(keys[5], 71), 0),
        "norm_gain": jnp.clip(1.0 + 0.18 * jax.random.normal(keys[1], (D,), jnp.float32), 0.1, 1.9),
        "w_gate": bell_draw(keys[2], (D, FF), D ** -0.5, 0.0625, ((0, 8), (1, 96))),
        "w_up": bell_draw(keys[3], (D, FF), D ** -0.5, 0.0625, ((0, 8), (1, 96))),
        "w_down": bell_draw(keys[4], (FF, D), (FF // 8) ** -0.5, 0.109375, ((0, 96), (1, 8))),
    }


def reference(tokens, norm_gain, w_gate, w_up, w_down):
    stream = tokens
    for step in range(ITERS):
        wide = stream.astype(jnp.float32)
        squares = lax.optimization_barrier(jnp.mean(wide * wide, axis=1, keepdims=True))
        normed = (wide * lax.rsqrt(squares + 1e-05) * norm_gain).astype(jnp.bfloat16)
        gate = jnp.dot(normed, w_gate, preferred_element_type=jnp.float32)
        up = jnp.dot(normed, w_up, preferred_element_type=jnp.float32)
        hidden = (jax.nn.silu(gate) * up).astype(jnp.bfloat16)
        delta = jnp.dot(hidden, w_down, preferred_element_type=jnp.float32)
        stream = (wide + delta).astype(jnp.bfloat16)
    return stream
```

```python
import jax
import jax.numpy as jnp
from jax import lax
from jax.sharding import PartitionSpec as P

D = 8192
ITERS = 2


def on_device(tokens, norm_gain, w_gate, w_up, w_down):
    width = w_gate.shape[1]
    rows, feats = tokens.shape
    cols = lax.axis_size("col")
    heads = lax.axis_size("row")
    total = rows * cols
    paired = jnp.concatenate([w_gate, w_up], axis=1)
    mixed = tokens
    for step in range(ITERS):
        spread = jnp.broadcast_to(mixed[None], (cols, rows, feats))
        everyone = lax.all_to_all(spread, "col", 0, 0).reshape(total, feats)
        wide = everyone.astype(jnp.float32)
        squares = jnp.sum(wide * wide, axis=1, keepdims=True)
        high = lax.reduce_precision(squares, 8, 7)
        rest = squares - high
        lane = lax.broadcasted_iota(jnp.int32, (total, 128), 1)
        extra = jnp.where(lane == 0, high, jnp.where(lane == 1, rest, 0.0))
        gained = (wide * norm_gain).astype(jnp.bfloat16)
        partial_value = jnp.dot(gained, paired, preferred_element_type=jnp.float32)
        packed = jnp.concatenate([partial_value, extra], axis=1).astype(jnp.bfloat16)
        shares = lax.all_to_all(packed.reshape(heads, total // heads, -1), "row", 0, 0)
        share = jnp.sum(shares.astype(jnp.float32), axis=0)
        scale = lax.rsqrt((share[:, 2 * width] + share[:, 2 * width + 1]) / D + 1e-05)[:, None]
        gate = share[:, :width] * scale
        up = share[:, width : 2 * width] * scale
        hidden = lax.all_gather(
            (jax.nn.silu(gate) * up).astype(jnp.bfloat16), "row", axis=0, tiled=True
        )
        delta = jnp.dot(hidden, w_down, preferred_element_type=jnp.float32).astype(jnp.bfloat16)
        deltas = lax.all_to_all(delta.reshape(cols, rows, feats), "col", 0, 0)
        mixed = (
            mixed.astype(jnp.float32) + jnp.sum(deltas.astype(jnp.float32), axis=0)
        ).astype(jnp.bfloat16)
    return mixed


def solution(mesh):
    return jax.shard_map(
        on_device,
        mesh=mesh,
        in_specs=(P("col", "row"), P("row"), P("row", "col"), P("row", "col"), P("col", "row")),
        out_specs=P("col", "row"),
        check_vma=False,
    )
```

```python
import jax
import jax.numpy as jnp
from jax import lax
from jax.sharding import Mesh, PartitionSpec as P

D = 8192
ITERS = 2
HI, CORE, LO = 4, 2, 2
PAIR = ((0, 1), (1, 0))


def matmul(left, right):
    return jnp.dot(left, right, preferred_element_type=jnp.float32)


def on_device(tokens, norm_gain, w_gate, w_up, w_down):
    width = 2 * w_gate.shape[1]
    rows, feats = tokens.shape
    ring = lax.axis_size("ring")
    total = rows * ring
    half = total // CORE
    core = lax.axis_index("core")
    gate_far = lax.ppermute(w_gate, "lo", PAIR)
    up_far = lax.ppermute(w_up, "lo", PAIR)
    down_far = None
    mixed = tokens
    for step in range(ITERS):
        spread = jnp.broadcast_to(mixed[None], (ring, rows, feats))
        everyone = lax.all_to_all(spread, "ring", 0, 0)
        if step == 0:
            everyone, later = lax.optimization_barrier((everyone, w_down))
            down_far = lax.ppermute(later, "lo", PAIR)
        wide = everyone.reshape(total, feats).astype(jnp.float32)
        squares = jnp.sum(wide * wide, axis=1, keepdims=True)
        high = lax.reduce_precision(squares, 8, 7)
        lane = lax.broadcasted_iota(jnp.int32, (total, 128), 1)
        extra = jnp.where(lane == 0, high, jnp.where(lane == 1, squares - high, 0.0))
        gained = (wide * norm_gain).astype(jnp.bfloat16)
        packed = jnp.concatenate(
            [matmul(gained, w_gate), matmul(gained, gate_far), matmul(gained, w_up), matmul(gained, up_far), extra],
            axis=1,
        ).astype(jnp.bfloat16)
        both = lax.all_gather(packed, "core", axis=0)
        mine = lax.dynamic_slice_in_dim(both, core * half, half, axis=1)
        chip = jnp.sum(mine.astype(jnp.float32), axis=0)
        chip_squares = (chip[:, 2 * width] + chip[:, 2 * width + 1])[:, None]
        chip_high = lax.reduce_precision(chip_squares, 8, 7)
        lane = lax.broadcasted_iota(jnp.int32, (half, 128), 1)
        chip_extra = jnp.where(lane == 0, chip_high, jnp.where(lane == 1, chip_squares - chip_high, 0.0))
        chip = jnp.concatenate([chip[:, : 2 * width], chip_extra], axis=1).astype(jnp.bfloat16)
        chips = lax.all_to_all(jnp.broadcast_to(chip[None], (HI,) + chip.shape), "hi", 0, 0)
        share = jnp.sum(chips.astype(jnp.float32), axis=0)
        scale = lax.rsqrt((share[:, 2 * width] + share[:, 2 * width + 1]) / D + 1e-05)[:, None]
        gate = share[:, :width] * scale
        up = share[:, width : 2 * width] * scale
        hidden = lax.all_gather(
            (jax.nn.silu(gate) * up).astype(jnp.bfloat16), "core", axis=0, tiled=True
        )
        near = width // LO
        delta = matmul(hidden[:, :near], w_down) + matmul(hidden[:, near:], down_far)
        deltas = lax.all_to_all(delta.astype(jnp.bfloat16).reshape(ring, rows, feats), "ring", 0, 0)
        mixed = (
            mixed.astype(jnp.float32) + jnp.sum(deltas.astype(jnp.float32), axis=0)
        ).astype(jnp.bfloat16)
    return mixed


def solution(mesh):
    ring = mesh.shape["col"] // LO
    fine = Mesh(mesh.devices.reshape(HI, CORE, LO, ring), ("hi", "core", "lo", "ring"))
    row, col = ("hi", "core"), ("lo", "ring")
    return jax.shard_map(
        on_device,
        mesh=fine,
        in_specs=(P(col, row), P(row), P(row, col), P(row, col), P(col, row)),
        out_specs=P(col, row),
        check_vma=False,
    )
```

```python
import jax
import jax.numpy as jnp
from jax import lax
from jax.sharding import Mesh, PartitionSpec as P

D = 8192
ITERS = 2
HI, CORE, LO = 4, 2, 2
PAIR = ((0, 1), (1, 0))


def matmul(left, right):
    return jnp.dot(left, right, preferred_element_type=jnp.float32)


def on_device(tokens, norm_gain, w_gate, w_up, w_down):
    width = 2 * w_gate.shape[1]
    rows, feats = tokens.shape
    ring = lax.axis_size("ring")
    total = rows * ring
    half = total // CORE
    core = lax.axis_index("core")
    paired = jnp.concatenate([w_gate, w_up], axis=1)
    far = lax.ppermute(paired, "lo", PAIR)
    down_far = None
    mixed = tokens
    for step in range(ITERS):
        spread = jnp.broadcast_to(mixed[None], (ring, rows, feats))
        everyone = lax.all_to_all(spread, "ring", 0, 0)
        if step == 0:
            everyone, later = lax.optimization_barrier((everyone, w_down))
            down_far = lax.ppermute(later, "lo", PAIR)
        wide = everyone.reshape(total, feats).astype(jnp.float32)
        squares = jnp.sum(wide * wide, axis=1, keepdims=True)
        gained = (wide * norm_gain).astype(jnp.bfloat16)
        packed = jnp.concatenate(
            [
                matmul(gained, paired).astype(jnp.bfloat16),
                matmul(gained, far).astype(jnp.bfloat16),
                jnp.broadcast_to(squares, (total, 128)).astype(jnp.bfloat16),
            ],
            axis=1,
        )
        both = lax.all_gather(packed, "core", axis=0)
        mine = lax.dynamic_slice_in_dim(both, core * half, half, axis=1)
        chip = jnp.sum(mine.astype(jnp.float32), axis=0).astype(jnp.bfloat16)
        share = jnp.sum(lax.all_gather(chip, "hi", axis=0).astype(jnp.float32), axis=0)
        scale = lax.rsqrt(share[:, 2 * width : 2 * width + 1] / D + 1e-05)
        near = width // LO
        sides = []
        for base in (0, width):
            gate = share[:, base : base + near] * scale
            up = share[:, base + near : base + width] * scale
            sides.append((jax.nn.silu(gate) * up).astype(jnp.bfloat16))
        hidden = lax.all_gather(jnp.concatenate(sides, axis=1), "core", axis=0, tiled=True)
        delta = matmul(hidden[:, :near], w_down) + matmul(hidden[:, near:], down_far)
        deltas = lax.all_to_all(delta.astype(jnp.bfloat16).reshape(ring, rows, feats), "ring", 0, 0)
        mixed = (
            mixed.astype(jnp.float32) + jnp.sum(deltas.astype(jnp.float32), axis=0)
        ).astype(jnp.bfloat16)
    return mixed


def solution(mesh):
    ring = mesh.shape["col"] // LO
    fine = Mesh(mesh.devices.reshape(HI, CORE, LO, ring), ("hi", "core", "lo", "ring"))
    row, col = ("hi", "core"), ("lo", "ring")
    return jax.shard_map(
        on_device,
        mesh=fine,
        in_specs=(P(col, row), P(row), P(row, col), P(row, col), P(col, row)),
        out_specs=P(col, row),
        check_vma=False,
    )
```

```python
import jax
import jax.numpy as jnp
from jax import lax
from jax.sharding import Mesh, PartitionSpec as P

D = 8192
ITERS = 2
HI, CORE, LO = 4, 2, 2
PAIR = ((0, 1), (1, 0))


def matmul(left, right):
    return jnp.dot(left, right, preferred_element_type=jnp.float32)


def on_device(tokens, norm_gain, w_gate, w_up, w_down):
    width = 2 * w_gate.shape[1]
    rows, feats = tokens.shape
    ring = lax.axis_size("ring")
    total = rows * ring
    half = total // CORE
    core = lax.axis_index("core")
    paired = jnp.concatenate([w_gate, w_up], axis=1)
    far = lax.ppermute(paired, "lo", PAIR)
    down_far = lax.ppermute(w_down, "lo", PAIR)
    mixed = tokens
    for step in range(ITERS):
        spread = jnp.broadcast_to(mixed[None], (ring, rows, feats))
        everyone = lax.all_to_all(spread, "ring", 0, 0)
        everyone = lax.optimization_barrier(everyone.reshape(total, feats))
        wide = everyone.astype(jnp.float32)
        squares = jnp.sum(wide * wide, axis=1, keepdims=True)
        gained = (wide * norm_gain).astype(jnp.bfloat16)
        packed = jnp.concatenate(
            [
                matmul(gained, paired).astype(jnp.bfloat16),
                matmul(gained, far).astype(jnp.bfloat16),
                jnp.broadcast_to(squares, (total, 128)).astype(jnp.bfloat16),
            ],
            axis=1,
        )
        both = lax.all_gather(packed, "core", axis=0)
        mine = lax.dynamic_slice_in_dim(both, core * half, half, axis=1)
        chip = jnp.sum(mine.astype(jnp.float32), axis=0).astype(jnp.bfloat16)
        share = jnp.sum(lax.all_gather(chip, "hi", axis=0).astype(jnp.float32), axis=0)
        scale = lax.rsqrt(share[:, 2 * width : 2 * width + 1] / D + 1e-05)
        near = width // LO
        sides = []
        for base in (0, width):
            gate = share[:, base : base + near] * scale
            up = share[:, base + near : base + width] * scale
            sides.append((jax.nn.silu(gate) * up).astype(jnp.bfloat16))
        hidden = lax.all_gather(jnp.concatenate(sides, axis=1), "core", axis=0, tiled=True)
        delta = matmul(hidden[:, :near], w_down) + matmul(hidden[:, near:], down_far)
        deltas = lax.all_to_all(delta.astype(jnp.bfloat16).reshape(ring, rows, feats), "ring", 0, 0)
        mixed = (
            mixed.astype(jnp.float32) + jnp.sum(deltas.astype(jnp.float32), axis=0)
        ).astype(jnp.bfloat16)
    return mixed


def solution(mesh):
    ring = mesh.shape["col"] // LO
    fine = Mesh(mesh.devices.reshape(HI, CORE, LO, ring), ("hi", "core", "lo", "ring"))
    row, col = ("hi", "core"), ("lo", "ring")
    return jax.shard_map(
        on_device,
        mesh=fine,
        in_specs=(P(col, row), P(row), P(row, col), P(row, col), P(col, row)),
        out_specs=P(col, row),
        check_vma=False,
    )
```

```python
import jax
import jax.numpy as jnp
from jax import lax
from jax.sharding import Mesh, PartitionSpec as P

D = 8192
ITERS = 2
HI, CORE, LO = 4, 2, 2
PAIR = ((0, 1), (1, 0))


def matmul(left, right):
    return jnp.dot(left, right, preferred_element_type=jnp.float32)


def on_device(tokens, norm_gain, w_gate, w_up, w_down):
    width = 2 * w_gate.shape[1]
    rows, feats = tokens.shape
    ring = lax.axis_size("ring")
    total = rows * ring
    half = total // CORE
    core = lax.axis_index("core")
    paired = jnp.concatenate([w_gate, w_up], axis=1)
    deep = w_down.shape[0]
    stripes = jnp.concatenate(jnp.split(w_down, feats // deep, axis=1), axis=0)
    swapped = lax.ppermute(jnp.concatenate([paired, stripes], axis=1), "lo", PAIR)
    far = swapped[:, :width]
    down_far = jnp.concatenate(jnp.split(swapped[:, width:], feats // deep, axis=0), axis=1)
    mixed = tokens
    for step in range(ITERS):
        spread = jnp.broadcast_to(mixed[None], (ring, rows, feats))
        everyone = lax.all_to_all(spread, "ring", 0, 0)
        everyone = lax.optimization_barrier(everyone.reshape(total, feats))
        wide = everyone.astype(jnp.float32)
        squares = jnp.sum(wide * wide, axis=1, keepdims=True)
        gained = (wide * norm_gain).astype(jnp.bfloat16)
        packed = jnp.concatenate(
            [
                matmul(gained, paired).astype(jnp.bfloat16),
                matmul(gained, far).astype(jnp.bfloat16),
                jnp.broadcast_to(squares, (total, 128)).astype(jnp.bfloat16),
            ],
            axis=1,
        )
        both = lax.all_gather(packed, "core", axis=0)
        mine = lax.dynamic_slice_in_dim(both, core * half, half, axis=1)
        chip = jnp.sum(mine.astype(jnp.float32), axis=0).astype(jnp.bfloat16)
        share = jnp.sum(lax.all_gather(chip, "hi", axis=0).astype(jnp.float32), axis=0)
        scale = lax.rsqrt(share[:, 2 * width : 2 * width + 1] / D + 1e-05)
        near = width // LO
        sides = []
        for base in (0, width):
            gate = share[:, base : base + near] * scale
            up = share[:, base + near : base + width] * scale
            sides.append((jax.nn.silu(gate) * up).astype(jnp.bfloat16))
        hidden = lax.all_gather(jnp.concatenate(sides, axis=1), "core", axis=0, tiled=True)
        delta = matmul(hidden[:, :near], w_down) + matmul(hidden[:, near:], down_far)
        deltas = lax.all_to_all(delta.astype(jnp.bfloat16).reshape(ring, rows, feats), "ring", 0, 0)
        mixed = (
            mixed.astype(jnp.float32) + jnp.sum(deltas.astype(jnp.float32), axis=0)
        ).astype(jnp.bfloat16)
    return mixed


def solution(mesh):
    ring = mesh.shape["col"] // LO
    fine = Mesh(mesh.devices.reshape(HI, CORE, LO, ring), ("hi", "core", "lo", "ring"))
    row, col = ("hi", "core"), ("lo", "ring")
    return jax.shard_map(
        on_device,
        mesh=fine,
        in_specs=(P(col, row), P(row), P(row, col), P(row, col), P(col, row)),
        out_specs=P(col, row),
        check_vma=False,
    )
```

```python
import jax
import jax.numpy as jnp
from jax import lax
from jax.sharding import Mesh, PartitionSpec as P

D = 8192
ITERS = 2
HI, CORE, FAR, NEAR = 4, 2, 2, 2
RING = ("yz", "near")
PAIR = ((0, 1), (1, 0))


def matmul(left, right):
    return jnp.dot(left, right, preferred_element_type=jnp.float32)


def on_device(tokens, norm_gain, w_gate, w_up, w_down):
    width = 2 * w_gate.shape[1]
    rows, feats = tokens.shape
    ring = lax.axis_size(RING)
    total = rows * ring
    half = total // CORE
    core = lax.axis_index("core")
    paired = jnp.concatenate([w_gate, w_up], axis=1)
    far = lax.ppermute(paired, "far", PAIR)
    down_far = lax.ppermute(w_down, "far", PAIR)
    mixed = tokens
    for step in range(ITERS):
        spread = jnp.broadcast_to(mixed[None], (ring, rows, feats))
        everyone = lax.all_to_all(spread, RING, 0, 0)
        everyone = lax.optimization_barrier(everyone.reshape(total, feats))
        wide = everyone.astype(jnp.float32)
        squares = jnp.sum(wide * wide, axis=1, keepdims=True)
        gained = (wide * norm_gain).astype(jnp.bfloat16)
        packed = jnp.concatenate(
            [
                matmul(gained, paired).astype(jnp.bfloat16),
                matmul(gained, far).astype(jnp.bfloat16),
                jnp.broadcast_to(squares, (total, 128)).astype(jnp.bfloat16),
            ],
            axis=1,
        )
        both = lax.all_gather(packed, "core", axis=0)
        mine = lax.dynamic_slice_in_dim(both, core * half, half, axis=1)
        chip = jnp.sum(mine.astype(jnp.float32), axis=0).astype(jnp.bfloat16)
        share = jnp.sum(lax.all_gather(chip, "hi", axis=0).astype(jnp.float32), axis=0)
        scale = lax.rsqrt(share[:, 2 * width : 2 * width + 1] / D + 1e-05)
        side = width // FAR
        sides = []
        for base in (0, width):
            gate = share[:, base : base + side] * scale
            up = share[:, base + side : base + width] * scale
            sides.append((jax.nn.silu(gate) * up).astype(jnp.bfloat16))
        hidden = lax.all_gather(jnp.concatenate(sides, axis=1), "core", axis=0, tiled=True)
        delta = matmul(hidden[:, :side], w_down) + matmul(hidden[:, side:], down_far)
        deltas = lax.all_to_all(delta.astype(jnp.bfloat16).reshape(ring, rows, feats), RING, 0, 0)
        mixed = (
            mixed.astype(jnp.float32) + jnp.sum(deltas.astype(jnp.float32), axis=0)
        ).astype(jnp.bfloat16)
    return mixed


def solution(mesh):
    planes = mesh.shape["col"] // (FAR * NEAR)
    fine = Mesh(mesh.devices.reshape(HI, CORE, planes, FAR, NEAR), ("hi", "core", "yz", "far", "near"))
    row, col = ("hi", "core"), ("yz", "far", "near")
    return jax.shard_map(
        on_device,
        mesh=fine,
        in_specs=(P(col, row), P(row), P(row, col), P(row, col), P(col, row)),
        out_specs=P(col, row),
        check_vma=False,
    )
```

```python
import jax
import jax.numpy as jnp
from jax import lax
from jax.sharding import Mesh, PartitionSpec as P

D = 8192
ITERS = 2
HI, CORE, LO = 4, 2, 2
PAIR = ((0, 1), (1, 0))


def matmul(left, right):
    return jnp.dot(left, right, preferred_element_type=jnp.float32)


def on_device(tokens, norm_gain, w_gate, w_up, w_down):
    width = 2 * w_gate.shape[1]
    rows, feats = tokens.shape
    ring = lax.axis_size("ring")
    total = rows * ring
    half = total // CORE
    core = lax.axis_index("core")
    deep = w_down.shape[0]
    block = jnp.zeros((feats, width + deep), w_gate.dtype)
    block = lax.dynamic_update_slice(block, w_gate, (0, 0))
    block = lax.dynamic_update_slice(block, w_up, (0, deep))
    for stripe in range(feats // deep):
        part = w_down[:, stripe * deep : (stripe + 1) * deep]
        block = lax.dynamic_update_slice(block, part, (stripe * deep, width))
    swapped = lax.ppermute(block, "lo", PAIR)
    paired, far = block[:, :width], swapped[:, :width]
    down_far = jnp.split(swapped[:, width:], feats // deep, axis=0)
    mixed = tokens
    for step in range(ITERS):
        spread = jnp.broadcast_to(mixed[None], (ring, rows, feats))
        everyone = lax.all_to_all(spread, "ring", 0, 0)
        everyone = lax.optimization_barrier(everyone.reshape(total, feats))
        wide = everyone.astype(jnp.float32)
        squares = jnp.sum(wide * wide, axis=1, keepdims=True)
        gained = (wide * norm_gain).astype(jnp.bfloat16)
        packed = jnp.concatenate(
            [
                matmul(gained, paired).astype(jnp.bfloat16),
                matmul(gained, far).astype(jnp.bfloat16),
                jnp.broadcast_to(squares, (total, 128)).astype(jnp.bfloat16),
            ],
            axis=1,
        )
        both = lax.all_gather(packed, "core", axis=0)
        mine = lax.dynamic_slice_in_dim(both, core * half, half, axis=1)
        chip = jnp.sum(mine.astype(jnp.float32), axis=0).astype(jnp.bfloat16)
        share = jnp.sum(lax.all_gather(chip, "hi", axis=0).astype(jnp.float32), axis=0)
        scale = lax.rsqrt(share[:, 2 * width : 2 * width + 1] / D + 1e-05)
        near = width // LO
        sides = []
        for base in (0, width):
            gate = share[:, base : base + near] * scale
            up = share[:, base + near : base + width] * scale
            sides.append((jax.nn.silu(gate) * up).astype(jnp.bfloat16))
        hidden = lax.all_gather(jnp.concatenate(sides, axis=1), "core", axis=0, tiled=True)
        delta = matmul(hidden[:, :near], w_down) + jnp.concatenate(
            [matmul(hidden[:, near:], stripe) for stripe in down_far], axis=1
        )
        deltas = lax.all_to_all(delta.astype(jnp.bfloat16).reshape(ring, rows, feats), "ring", 0, 0)
        mixed = (
            mixed.astype(jnp.float32) + jnp.sum(deltas.astype(jnp.float32), axis=0)
        ).astype(jnp.bfloat16)
    return mixed


def solution(mesh):
    ring = mesh.shape["col"] // LO
    fine = Mesh(mesh.devices.reshape(HI, CORE, LO, ring), ("hi", "core", "lo", "ring"))
    row, col = ("hi", "core"), ("lo", "ring")
    return jax.shard_map(
        on_device,
        mesh=fine,
        in_specs=(P(col, row), P(row), P(row, col), P(row, col), P(col, row)),
        out_specs=P(col, row),
        check_vma=False,
    )
```

```python
import jax
import jax.numpy as jnp
from jax import lax
from jax.sharding import Mesh, PartitionSpec as P

D = 8192
ITERS = 2
HI, CORE, FAR, NEAR = 4, 2, 2, 2
RING = ("yz", "near")
PAIR = ((0, 1), (1, 0))


def matmul(left, right):
    return jnp.dot(left, right, preferred_element_type=jnp.float32)


def on_device(tokens, norm_gain, w_gate, w_up, w_down):
    width = 2 * w_gate.shape[1]
    rows, feats = tokens.shape
    ring = lax.axis_size(RING)
    total = rows * ring
    half = total // CORE
    core = lax.axis_index("core")
    paired = jnp.concatenate([w_gate, w_up], axis=1)
    far = lax.ppermute(paired, "far", PAIR)
    down_far = None
    mixed = tokens
    for step in range(ITERS):
        spread = jnp.broadcast_to(mixed[None], (ring, rows, feats))
        everyone = lax.all_to_all(spread, RING, 0, 0)
        if step == 0:
            everyone, later = lax.optimization_barrier((everyone.reshape(total, feats), w_down))
            down_far = lax.ppermute(later, "far", PAIR)
        else:
            everyone = lax.optimization_barrier(everyone.reshape(total, feats))
        wide = everyone.astype(jnp.float32)
        squares = jnp.sum(wide * wide, axis=1, keepdims=True)
        gained = (wide * norm_gain).astype(jnp.bfloat16)
        packed = jnp.concatenate(
            [
                matmul(gained, paired).astype(jnp.bfloat16),
                matmul(gained, far).astype(jnp.bfloat16),
                jnp.broadcast_to(squares, (total, 128)).astype(jnp.bfloat16),
            ],
            axis=1,
        )
        both = lax.all_gather(packed, "core", axis=0)
        mine = lax.dynamic_slice_in_dim(both, core * half, half, axis=1)
        chip = jnp.sum(mine.astype(jnp.float32), axis=0).astype(jnp.bfloat16)
        share = jnp.sum(lax.all_gather(chip, "hi", axis=0).astype(jnp.float32), axis=0)
        scale = lax.rsqrt(share[:, 2 * width : 2 * width + 1] / D + 1e-05)
        side = width // FAR
        sides = []
        for base in (0, width):
            gate = share[:, base : base + side] * scale
            up = share[:, base + side : base + width] * scale
            sides.append((jax.nn.silu(gate) * up).astype(jnp.bfloat16))
        hidden = lax.all_gather(jnp.concatenate(sides, axis=1), "core", axis=0, tiled=True)
        delta = matmul(hidden[:, :side], w_down) + matmul(hidden[:, side:], down_far)
        deltas = lax.all_to_all(delta.astype(jnp.bfloat16).reshape(ring, rows, feats), RING, 0, 0)
        mixed = (
            mixed.astype(jnp.float32) + jnp.sum(deltas.astype(jnp.float32), axis=0)
        ).astype(jnp.bfloat16)
    return mixed


def solution(mesh):
    planes = mesh.shape["col"] // (FAR * NEAR)
    fine = Mesh(mesh.devices.reshape(HI, CORE, planes, FAR, NEAR), ("hi", "core", "yz", "far", "near"))
    row, col = ("hi", "core"), ("yz", "far", "near")
    return jax.shard_map(
        on_device,
        mesh=fine,
        in_specs=(P(col, row), P(row), P(row, col), P(row, col), P(col, row)),
        out_specs=P(col, row),
        check_vma=False,
    )
```

```python
import jax
import jax.numpy as jnp
from jax import lax
from jax.sharding import Mesh, PartitionSpec as P

D = 8192
ITERS = 2
HI, CORE, LO, FAR, NEAR = 4, 2, 2, 2, 2
RING = ("near", "z", "far")
PAIR = ((0, 1), (1, 0))


def matmul(left, right):
    return jnp.dot(left, right, preferred_element_type=jnp.float32)


def on_device(tokens, norm_gain, w_gate, w_up, w_down):
    width = 2 * w_gate.shape[1]
    rows, feats = tokens.shape
    ring = lax.axis_size(RING)
    total = rows * ring
    half = total // CORE
    core = lax.axis_index("core")
    paired = jnp.concatenate([w_gate, w_up], axis=1)
    far = lax.ppermute(paired, "lo", PAIR)
    down_far = lax.ppermute(w_down, "lo", PAIR)
    mixed = tokens
    for step in range(ITERS):
        spread = jnp.broadcast_to(mixed[None], (ring, rows, feats))
        everyone = lax.all_to_all(spread, RING, 0, 0)
        everyone = lax.optimization_barrier(everyone.reshape(total, feats))
        wide = everyone.astype(jnp.float32)
        squares = jnp.sum(wide * wide, axis=1, keepdims=True)
        gained = (wide * norm_gain).astype(jnp.bfloat16)
        packed = jnp.concatenate(
            [
                matmul(gained, paired).astype(jnp.bfloat16),
                matmul(gained, far).astype(jnp.bfloat16),
                jnp.broadcast_to(squares, (total, 128)).astype(jnp.bfloat16),
            ],
            axis=1,
        )
        both = lax.all_gather(packed, "core", axis=0)
        mine = lax.dynamic_slice_in_dim(both, core * half, half, axis=1)
        chip = jnp.sum(mine.astype(jnp.float32), axis=0).astype(jnp.bfloat16)
        share = jnp.sum(lax.all_gather(chip, "hi", axis=0).astype(jnp.float32), axis=0)
        scale = lax.rsqrt(share[:, 2 * width : 2 * width + 1] / D + 1e-05)
        near = width // LO
        sides = []
        for base in (0, width):
            gate = share[:, base : base + near] * scale
            up = share[:, base + near : base + width] * scale
            sides.append((jax.nn.silu(gate) * up).astype(jnp.bfloat16))
        hidden = lax.all_gather(jnp.concatenate(sides, axis=1), "core", axis=0, tiled=True)
        delta = matmul(hidden[:, :near], w_down) + matmul(hidden[:, near:], down_far)
        deltas = lax.all_to_all(delta.astype(jnp.bfloat16).reshape(ring, rows, feats), RING, 0, 0)
        mixed = (
            mixed.astype(jnp.float32) + jnp.sum(deltas.astype(jnp.float32), axis=0)
        ).astype(jnp.bfloat16)
    return mixed


def solution(mesh):
    depth = mesh.shape["col"] // (LO * FAR * NEAR)
    fine = Mesh(mesh.devices.reshape(HI, CORE, LO, depth, FAR, NEAR), ("hi", "core", "lo", "z", "far", "near"))
    row, col = ("hi", "core"), ("lo", "z", "far", "near")
    return jax.shard_map(
        on_device,
        mesh=fine,
        in_specs=(P(col, row), P(row), P(row, col), P(row, col), P(col, row)),
        out_specs=P(col, row),
        check_vma=False,
    )
```

```python
import jax
import jax.numpy as jnp
from jax import lax
from jax.sharding import Mesh, PartitionSpec as P

D = 8192
ITERS = 2
HI, CORE, LO, FAR, NEAR = 4, 2, 2, 2, 2
RING = ("near", "z", "far")
PAIR = ((0, 1), (1, 0))


def matmul(left, right):
    return jnp.dot(left, right, preferred_element_type=jnp.float32)


def partial_sums(rows_in, norm_gain, blocks):
    wide = rows_in.astype(jnp.float32)
    squares = jnp.sum(wide * wide, axis=1, keepdims=True)
    gained = (wide * norm_gain).astype(jnp.bfloat16)
    parts = [matmul(gained, block).astype(jnp.bfloat16) for block in blocks]
    parts.append(jnp.broadcast_to(squares, (rows_in.shape[0], 128)).astype(jnp.bfloat16))
    return jnp.concatenate(parts, axis=1)


def hidden_units(packed, side):
    half = packed.shape[0] // CORE
    both = lax.all_gather(packed, "core", axis=0)
    mine = lax.dynamic_slice_in_dim(both, lax.axis_index("core") * half, half, axis=1)
    chip = jnp.sum(mine.astype(jnp.float32), axis=0).astype(jnp.bfloat16)
    share = jnp.sum(lax.all_gather(chip, "hi", axis=0).astype(jnp.float32), axis=0)
    last = share.shape[1] - 128
    scale = lax.rsqrt(share[:, last : last + 1] / D + 1e-05)
    units = []
    for base in range(0, last, 2 * side):
        gate = share[:, base : base + side] * scale
        up = share[:, base + side : base + 2 * side] * scale
        units.append((jax.nn.silu(gate) * up).astype(jnp.bfloat16))
    return jnp.concatenate(units, axis=1)


def on_device(tokens, norm_gain, w_gate, w_up, w_down):
    side = w_gate.shape[1]
    rows, feats = tokens.shape
    ring = lax.axis_size(RING)
    total = rows * ring
    lo = lax.axis_index("lo")
    paired = jnp.concatenate([w_gate, w_up], axis=1)
    down_far = lax.ppermute(w_down, "lo", PAIR)
    far = None
    mixed = tokens
    for step in range(ITERS):
        spread = jnp.broadcast_to(mixed[None], (ring, rows, feats))
        everyone = lax.all_to_all(spread, RING, 0, 0).reshape(total, feats)
        if step == 0:
            everyone = lax.optimization_barrier(lax.all_gather(everyone, "lo", axis=0, tiled=True))
            units = hidden_units(partial_sums(everyone, norm_gain, [paired]), side)
            blocks = lax.all_gather(units, ("core", "lo"), axis=0)
            near = lax.dynamic_index_in_dim(blocks, lo * LO + lo, 0, keepdims=False)
            other = lax.dynamic_index_in_dim(blocks, lo * LO + 1 - lo, 0, keepdims=False)
        else:
            everyone = lax.optimization_barrier(everyone)
            units = hidden_units(partial_sums(everyone, norm_gain, [paired, far]), side)
            hidden = lax.all_gather(units, "core", axis=0, tiled=True)
            near, other = hidden[:, :side], hidden[:, side:]
        delta = (matmul(near, w_down) + matmul(other, down_far)).astype(jnp.bfloat16)
        if step == 0:
            delta, later = lax.optimization_barrier((delta, paired))
            far = lax.ppermute(later, "lo", PAIR)
        deltas = lax.all_to_all(delta.reshape(ring, rows, feats), RING, 0, 0)
        mixed = (
            mixed.astype(jnp.float32) + jnp.sum(deltas.astype(jnp.float32), axis=0)
        ).astype(jnp.bfloat16)
    return mixed


def solution(mesh):
    depth = mesh.shape["col"] // (LO * FAR * NEAR)
    fine = Mesh(mesh.devices.reshape(HI, CORE, LO, depth, FAR, NEAR), ("hi", "core", "lo", "z", "far", "near"))
    row, col = ("hi", "core"), ("lo", "z", "far", "near")
    return jax.shard_map(
        on_device,
        mesh=fine,
        in_specs=(P(col, row), P(row), P(row, col), P(row, col), P(col, row)),
        out_specs=P(col, row),
        check_vma=False,
    )
```

```python
import jax
import jax.numpy as jnp
from jax import lax
from jax.sharding import Mesh, PartitionSpec as P

D = 8192
ITERS = 2
HI, CORE, LO, FAR, NEAR = 4, 2, 2, 2, 2
RING = ("near", "z", "far")
PAIR = ((0, 1), (1, 0))


def matmul(left, right):
    return jnp.dot(left, right, preferred_element_type=jnp.float32)


def on_device(tokens, norm_gain, w_gate, w_up, w_down):
    width = 2 * w_gate.shape[1]
    rows, feats = tokens.shape
    ring = lax.axis_size(RING)
    total = rows * ring
    half = total // CORE
    core = lax.axis_index("core")
    paired = jnp.concatenate([w_gate, w_up], axis=1)
    far = lax.ppermute(paired, "lo", PAIR)
    down_far = None
    mixed = tokens
    for step in range(ITERS):
        spread = jnp.broadcast_to(mixed[None], (ring, rows, feats))
        everyone = lax.all_to_all(spread, RING, 0, 0)
        if step == 0:
            everyone, later = lax.optimization_barrier((everyone.reshape(total, feats), w_down))
            down_far = lax.ppermute(later, "lo", PAIR)
        else:
            everyone = lax.optimization_barrier(everyone.reshape(total, feats))
        wide = everyone.astype(jnp.float32)
        squares = jnp.sum(wide * wide, axis=1, keepdims=True)
        gained = (wide * norm_gain).astype(jnp.bfloat16)
        packed = jnp.concatenate(
            [
                matmul(gained, paired).astype(jnp.bfloat16),
                matmul(gained, far).astype(jnp.bfloat16),
                jnp.broadcast_to(squares, (total, 128)).astype(jnp.bfloat16),
            ],
            axis=1,
        )
        both = lax.all_gather(packed, "core", axis=0)
        mine = lax.dynamic_slice_in_dim(both, core * half, half, axis=1)
        chip = jnp.sum(mine.astype(jnp.float32), axis=0).astype(jnp.bfloat16)
        share = jnp.sum(lax.all_gather(chip, "hi", axis=0).astype(jnp.float32), axis=0)
        scale = lax.rsqrt(share[:, 2 * width : 2 * width + 1] / D + 1e-05)
        near = width // LO
        sides = []
        for base in (0, width):
            gate = share[:, base : base + near] * scale
            up = share[:, base + near : base + width] * scale
            sides.append((jax.nn.silu(gate) * up).astype(jnp.bfloat16))
        hidden = lax.all_gather(jnp.concatenate(sides, axis=1), "core", axis=0, tiled=True)
        delta = matmul(hidden[:, :near], w_down) + matmul(hidden[:, near:], down_far)
        deltas = lax.all_to_all(delta.astype(jnp.bfloat16).reshape(ring, rows, feats), RING, 0, 0)
        mixed = (
            mixed.astype(jnp.float32) + jnp.sum(deltas.astype(jnp.float32), axis=0)
        ).astype(jnp.bfloat16)
    return mixed


def solution(mesh):
    depth = mesh.shape["col"] // (LO * FAR * NEAR)
    fine = Mesh(mesh.devices.reshape(HI, CORE, LO, depth, FAR, NEAR), ("hi", "core", "lo", "z", "far", "near"))
    row, col = ("hi", "core"), ("lo", "z", "far", "near")
    return jax.shard_map(
        on_device,
        mesh=fine,
        in_specs=(P(col, row), P(row), P(row, col), P(row, col), P(col, row)),
        out_specs=P(col, row),
        check_vma=False,
    )
```

```python
import jax
import jax.numpy as jnp
from jax import lax
from jax.sharding import Mesh, PartitionSpec as P

D = 8192
ITERS = 2
HI, CORE, FAR, NEAR = 4, 2, 2, 2
RING = ("yz", "near")
PAIR = ((0, 1), (1, 0))


def matmul(left, right):
    return jnp.dot(left, right, preferred_element_type=jnp.float32)


def on_device(tokens, norm_gain, w_gate, w_up, w_down):
    width = 2 * w_gate.shape[1]
    rows, feats = tokens.shape
    ring = lax.axis_size(RING)
    total = rows * ring
    half = total // CORE
    core = lax.axis_index("core")
    paired = jnp.concatenate([w_gate, w_up], axis=1)
    far = lax.ppermute(paired, "far", PAIR)
    down_far = lax.ppermute(w_down, "far", PAIR)
    mixed = tokens
    for step in range(ITERS):
        spread = jnp.broadcast_to(mixed[None], (ring, rows, feats))
        everyone = lax.all_to_all(spread, RING, 0, 0)
        everyone = lax.optimization_barrier(everyone.reshape(total, feats))
        wide = everyone.astype(jnp.float32)
        squares = jnp.sum(wide * wide, axis=1)
        gained = (wide * norm_gain).astype(jnp.bfloat16)
        line = jnp.broadcast_to(jnp.pad(squares, (0, feats - total))[None], (8, feats))
        parts = jnp.concatenate([matmul(gained, paired), matmul(gained, far)], axis=1)
        packed = jnp.concatenate([parts.astype(jnp.bfloat16), line.astype(jnp.bfloat16)], axis=0)
        both = lax.all_gather(packed, "core", axis=0)
        mine = lax.dynamic_slice_in_dim(both, core * half, half, axis=1)
        chip = jnp.sum(mine.astype(jnp.float32), axis=0).astype(jnp.bfloat16)
        chip_line = jnp.sum(both[:, total:, :128].astype(jnp.float32), axis=0).astype(jnp.bfloat16)
        stacked = jnp.concatenate(jnp.split(chip, 2 * width // 128, axis=1) + [chip_line], axis=0)
        share = jnp.sum(lax.all_gather(stacked, "hi", axis=0).astype(jnp.float32), axis=0)
        all_squares = share[share.shape[0] - 1, :total]
        scale = lax.rsqrt(jnp.where(core == 0, all_squares[:half], all_squares[half:]) / D + 1e-05)[:, None]
        side = width // FAR
        pieces = side // 128
        sides = []
        for block in range(FAR):
            for piece in range(pieces):
                at = (2 * pieces * block + piece) * half
                gate = share[at : at + half] * scale
                up = share[at + pieces * half : at + (pieces + 1) * half] * scale
                sides.append((jax.nn.silu(gate) * up).astype(jnp.bfloat16))
        hidden = lax.all_gather(jnp.concatenate(sides, axis=1), "core", axis=0, tiled=True)
        delta = matmul(hidden[:, :side], w_down) + matmul(hidden[:, side:], down_far)
        deltas = lax.all_to_all(delta.astype(jnp.bfloat16).reshape(ring, rows, feats), RING, 0, 0)
        mixed = (
            mixed.astype(jnp.float32) + jnp.sum(deltas.astype(jnp.float32), axis=0)
        ).astype(jnp.bfloat16)
    return mixed


def solution(mesh):
    planes = mesh.shape["col"] // (FAR * NEAR)
    fine = Mesh(mesh.devices.reshape(HI, CORE, planes, FAR, NEAR), ("hi", "core", "yz", "far", "near"))
    row, col = ("hi", "core"), ("yz", "far", "near")
    return jax.shard_map(
        on_device,
        mesh=fine,
        in_specs=(P(col, row), P(row), P(row, col), P(row, col), P(col, row)),
        out_specs=P(col, row),
        check_vma=False,
    )
```

```python
import jax
import jax.numpy as jnp
from jax import lax
from jax.sharding import Mesh, PartitionSpec as P

D = 8192
ITERS = 2
HI, CORE, FAR, NEAR = 4, 2, 2, 2
RING = ("yz", "near")
PAIR = ((0, 1), (1, 0))


def matmul(left, right):
    return jnp.dot(left, right, preferred_element_type=jnp.float32)


def on_device(tokens, norm_gain, w_gate, w_up, w_down):
    width = 2 * w_gate.shape[1]
    rows, feats = tokens.shape
    ring = lax.axis_size(RING)
    total = rows * ring
    half = total // CORE
    core = lax.axis_index("core")
    paired = jnp.concatenate([w_gate, w_up], axis=1)
    far = lax.ppermute(paired, "far", PAIR)
    down_far = lax.ppermute(w_down, "far", PAIR)
    gain = lax.optimization_barrier(jnp.broadcast_to(norm_gain[None], (8, feats)))
    mixed = tokens
    for step in range(ITERS):
        spread = jnp.broadcast_to(mixed[None], (ring, rows, feats))
        everyone = lax.all_to_all(spread, RING, 0, 0)
        everyone = lax.optimization_barrier(everyone.reshape(total, feats))
        wide = everyone.astype(jnp.float32)
        squares = jnp.sum(wide * wide, axis=1)
        gained = (wide * gain[:1]).astype(jnp.bfloat16)
        line = jnp.broadcast_to(jnp.pad(squares, (0, feats - total))[None], (8, feats))
        parts = jnp.concatenate([matmul(gained, paired), matmul(gained, far)], axis=1)
        packed = jnp.concatenate([parts.astype(jnp.bfloat16), line.astype(jnp.bfloat16)], axis=0)
        both = lax.all_gather(packed, "core", axis=0)
        mine = lax.dynamic_slice_in_dim(both, core * half, half, axis=1)
        chip = jnp.sum(mine.astype(jnp.float32), axis=0).astype(jnp.bfloat16)
        chip_line = jnp.sum(both[:, total:, :128].astype(jnp.float32), axis=0).astype(jnp.bfloat16)
        stacked = jnp.concatenate(jnp.split(chip, 2 * width // 128, axis=1) + [chip_line], axis=0)
        share = jnp.sum(lax.all_gather(stacked, "hi", axis=0).astype(jnp.float32), axis=0)
        all_squares = share[share.shape[0] - 1, :total]
        scale = lax.rsqrt(jnp.where(core == 0, all_squares[:half], all_squares[half:]) / D + 1e-05)[:, None]
        side = width // FAR
        pieces = side // 128
        sides = []
        for block in range(FAR):
            for piece in range(pieces):
                at = (2 * pieces * block + piece) * half
                gate = share[at : at + half] * scale
                up = share[at + pieces * half : at + (pieces + 1) * half] * scale
                sides.append((jax.nn.silu(gate) * up).astype(jnp.bfloat16))
        hidden = lax.all_gather(jnp.concatenate(sides, axis=1), "core", axis=0, tiled=True)
        delta = matmul(hidden[:, :side], w_down) + matmul(hidden[:, side:], down_far)
        deltas = lax.all_to_all(delta.astype(jnp.bfloat16).reshape(ring, rows, feats), RING, 0, 0)
        mixed = (
            mixed.astype(jnp.float32) + jnp.sum(deltas.astype(jnp.float32), axis=0)
        ).astype(jnp.bfloat16)
    return mixed


def solution(mesh):
    planes = mesh.shape["col"] // (FAR * NEAR)
    fine = Mesh(mesh.devices.reshape(HI, CORE, planes, FAR, NEAR), ("hi", "core", "yz", "far", "near"))
    row, col = ("hi", "core"), ("yz", "far", "near")
    return jax.shard_map(
        on_device,
        mesh=fine,
        in_specs=(P(col, row), P(row), P(row, col), P(row, col), P(col, row)),
        out_specs=P(col, row),
        check_vma=False,
    )
```

```python
import jax
import jax.numpy as jnp
from jax import lax
from jax.sharding import Mesh, PartitionSpec as P

D = 8192
ITERS = 2
HI, CORE, LO, FAR, NEAR = 4, 2, 2, 2, 2
RING = ("near", "z", "far")
PAIR = ((0, 1), (1, 0))


def matmul(left, right):
    return jnp.dot(left, right, preferred_element_type=jnp.float32)


def on_device(tokens, norm_gain, w_gate, w_up, w_down):
    width = 2 * w_gate.shape[1]
    rows, feats = tokens.shape
    ring = lax.axis_size(RING)
    total = rows * ring
    half = total // CORE
    core = lax.axis_index("core")
    paired = jnp.concatenate([w_gate, w_up], axis=1)
    far = lax.ppermute(paired, "lo", PAIR)
    down_far = lax.ppermute(w_down, "lo", PAIR)
    gain = lax.optimization_barrier(jnp.broadcast_to(norm_gain[None], (8, feats)))
    mixed = tokens
    for step in range(ITERS):
        spread = jnp.broadcast_to(mixed[None], (ring, rows, feats))
        everyone = lax.all_to_all(spread, RING, 0, 0)
        everyone = lax.optimization_barrier(everyone.reshape(total, feats))
        wide = everyone.astype(jnp.float32)
        squares = jnp.sum(wide * wide, axis=1)
        gained = (wide * gain[:1]).astype(jnp.bfloat16)
        line = jnp.broadcast_to(jnp.pad(squares, (0, feats - total))[None], (8, feats))
        parts = jnp.concatenate([matmul(gained, paired), matmul(gained, far)], axis=1)
        packed = jnp.concatenate([parts.astype(jnp.bfloat16), line.astype(jnp.bfloat16)], axis=0)
        both = lax.all_gather(packed, "core", axis=0)
        mine = lax.dynamic_slice_in_dim(both, core * half, half, axis=1)
        chip = jnp.sum(mine.astype(jnp.float32), axis=0).astype(jnp.bfloat16)
        chip_line = jnp.sum(both[:, total:, :128].astype(jnp.float32), axis=0).astype(jnp.bfloat16)
        stacked = jnp.concatenate(jnp.split(chip, 2 * width // 128, axis=1) + [chip_line], axis=0)
        share = jnp.sum(lax.all_gather(stacked, "hi", axis=0).astype(jnp.float32), axis=0)
        all_squares = share[share.shape[0] - 1, :total]
        scale = lax.rsqrt(jnp.where(core == 0, all_squares[:half], all_squares[half:]) / D + 1e-05)[:, None]
        side = width // LO
        pieces = side // 128
        sides = []
        for block in range(LO):
            for piece in range(pieces):
                at = (2 * pieces * block + piece) * half
                gate = share[at : at + half] * scale
                up = share[at + pieces * half : at + (pieces + 1) * half] * scale
                sides.append((jax.nn.silu(gate) * up).astype(jnp.bfloat16))
        hidden = lax.all_gather(jnp.concatenate(sides, axis=1), "core", axis=0, tiled=True)
        delta = matmul(hidden[:, :side], w_down) + matmul(hidden[:, side:], down_far)
        deltas = lax.all_to_all(delta.astype(jnp.bfloat16).reshape(ring, rows, feats), RING, 0, 0)
        mixed = (
            mixed.astype(jnp.float32) + jnp.sum(deltas.astype(jnp.float32), axis=0)
        ).astype(jnp.bfloat16)
    return mixed


def solution(mesh):
    depth = mesh.shape["col"] // (LO * FAR * NEAR)
    fine = Mesh(mesh.devices.reshape(HI, CORE, LO, depth, FAR, NEAR), ("hi", "core", "lo", "z", "far", "near"))
    row, col = ("hi", "core"), ("lo", "z", "far", "near")
    return jax.shard_map(
        on_device,
        mesh=fine,
        in_specs=(P(col, row), P(row), P(row, col), P(row, col), P(col, row)),
        out_specs=P(col, row),
        check_vma=False,
    )
```
